256 devices in a mesh: grp: 16 (over x_lo, z), inner: 16 (over y, x_hi, core).
Axes of the slice: x: 4 (x_hi: 2, x_lo: 2; x = x_hi * 2 + x_lo), y: 4, z: 8, core: 2. Of those that a mesh axis runs over, the one named last changes fastest.
Arguments:
- signal: bfloat16 [128, 1024, 4096], P('grp', None, 'inner'), may hold values from -6 to 6
- bins: int32 [8], replicated, may hold values from 1 to 512, as said below
- mic_positions: float32 [3, 4096], replicated, may hold values from -1 to 1
- grid_positions: float32 [3, 1024], replicated, may hold values from 1 to 3
Outputs:
- beam_map: float32 [8, 1024], replicated
The draws below stay inside these ranges and needn't reach their ends.
Inputs may be any that keep to these rules, and one draw needn't show every extreme that they name: The 8 bins are distinct; bin 1 and bin 1024 / 2 are always among them.
All inputs are finite; a program needn't handle non-finite values.
Results may differ from the reference program's by a relative error of at most 0.02.
Values may be sent and summed in bfloat16 or wider, within the bound.
A program may use at most 128 MiB of HBM per device.

```python
import math
import jax
import jax.numpy as jnp
from jax import lax

M = 4096
SAMPLES = 1024
F = 8
POINTS = 1024
SNAPS = 128


def draw_bins(key, part):
    inner_key = jax.random.fold_in(key, 11)
    order_key = jax.random.fold_in(key, 23)
    middle = jax.random.permutation(inner_key, SAMPLES // 2 - 2)[:F - 2] + 2
    ends = jnp.array([1, SAMPLES // 2], dtype=jnp.int32)
    chosen = jnp.concatenate([ends, middle.astype(jnp.int32)], 0)
    placing = jax.random.permutation(order_key, F)
    return chosen[placing].astype(jnp.int32)


def levels(own_key, shape, split, smallest, high):
    gain = 1.0
    for axis_at, shards_of in split:
        draws = jax.random.uniform(jax.random.fold_in(jax.random.fold_in(own_key, 6), axis_at), (shards_of,), jnp.float32, smallest / len(split), high / len(split))
        gain = gain * jnp.repeat(jnp.exp(draws), shape[axis_at] // shards_of).reshape((-1,) + (1,) * (len(shape) - 1 - axis_at))
    return gain


def normal_values(stream_key, dims, scale, bound, shards=(), held_as=jnp.bfloat16):
    level = levels(stream_key, dims, shards, -0.22, 0.18) if shards else 1.0
    drawn = jax.random.normal(stream_key, dims, jnp.float32) * scale * level
    return jnp.minimum(jnp.maximum(drawn, -bound), bound).astype(held_as)


def setup_inputs(seed: int = 0) -> dict:
    seeds = jax.random.split(jax.random.key(seed), 5)
    return {
        "signal": normal_values(seeds[0], (SNAPS, SAMPLES, M), 1.0, 6.0, ((0, 16), (2, 16))),
        "bins": draw_bins(jax.random.fold_in(seeds[4], 71), 0),
        "mic_positions": jnp.clip(jax.random.uniform(seeds[2], (3, M), jnp.float32, -1.0, 1.0), -1.0, 1.0),
        "grid_positions": jnp.clip(jax.random.uniform(seeds[3], (3, POINTS), jnp.float32, 1.0, 3.0), 1.0, 3.0),
    }


TWO_PI = 2.0 * math.pi
RATE_OVER_SOUND = 51200.0 / 343.0

def dft_table(bins):
    ticks = jnp.arange(SAMPLES, dtype=jnp.int32)
    turns = bins[:, None] * ticks[None, :] % SAMPLES
    angle = turns.astype(jnp.float32) * (TWO_PI / SAMPLES)
    window = 0.5 - 0.5 * jnp.cos(ticks.astype(jnp.float32) * (TWO_PI / SAMPLES))
    factor = math.sqrt(8.0 / (3.0 * SAMPLES))
    real_part = window[None, :] * jnp.cos(angle) * factor
    imag_part = -window[None, :] * jnp.sin(angle) * factor
    return jnp.concatenate([real_part, imag_part], 0).astype(jnp.bfloat16)

def distances(spots, grid):
    delta_x = grid[0][None, :] - spots[0][:, None]
    delta_y = grid[1][None, :] - spots[1][:, None]
    delta_z = grid[2][None, :] - spots[2][:, None]
    return jnp.sqrt(delta_x * delta_x + delta_y * delta_y + delta_z * delta_z) * RATE_OVER_SOUND

def steering(delay, frequency_bin):
    angle = delay * (frequency_bin.astype(jnp.float32) * (TWO_PI / SAMPLES))
    return jnp.concatenate([jnp.cos(angle), -jnp.sin(angle)], 0).astype(jnp.bfloat16)

def reference(signal, bins, mic_positions, grid_positions):
    table = dft_table(bins)

    def transform(block):
        return jnp.dot(table, block, preferred_element_type=jnp.float32).astype(jnp.bfloat16)
    spectra = lax.map(transform, signal).reshape(SNAPS, 2, F, M)
    delay = distances(mic_positions, grid_positions)
    diagonal_mask = jnp.eye(M, dtype=bool)

    def one_bin(index):
        real_x = spectra[:, 0, index, :]
        imag_x = spectra[:, 1, index, :]
        real_c = jnp.dot(real_x.T, real_x, preferred_element_type=jnp.float32) + jnp.dot(imag_x.T, imag_x, preferred_element_type=jnp.float32)
        imag_c = jnp.dot(imag_x.T, real_x, preferred_element_type=jnp.float32) - jnp.dot(real_x.T, imag_x, preferred_element_type=jnp.float32)
        real_c = jnp.where(diagonal_mask, 0.0, real_c / SNAPS)
        imag_c = jnp.where(diagonal_mask, 0.0, imag_c / SNAPS)
        block = jnp.concatenate([jnp.concatenate([real_c, -imag_c], 1), jnp.concatenate([imag_c, real_c], 1)], 0)
        steer = steering(delay, bins[index]).astype(jnp.float32)
        image = jnp.dot(block, steer, precision=lax.Precision.HIGHEST, preferred_element_type=jnp.float32)
        return lax.optimization_barrier(jnp.sum(steer * image, axis=0))
    partial_value = lax.map(one_bin, jnp.arange(F, dtype=jnp.int32))
    return partial_value * (math.sqrt(SNAPS) / M)
```

```python
import functools
import math

import jax
import jax.numpy as jnp
from jax import lax
from jax.experimental import pallas as pl
from jax.experimental.pallas import tpu as pltpu
from jax.sharding import PartitionSpec as P

SAMPLES = 1024
F = 8
X_LO = 2
TURNS_PER_METRE = (51200.0 / 343.0) / SAMPLES
MESH = pl.DeviceIdType.MESH

COS = (
    1.0,
    -19.73920440673828,
    64.93911743164062,
    -85.45014190673828,
    60.16762924194336,
    -25.967599868774414,
    6.528658390045166,
)
SIN = (
    6.283185005187988,
    -41.341590881347656,
    81.59994506835938,
    -76.61447143554688,
    41.3428840637207,
    -12.471243858337402,
)


def horner(coefficients, u):
    value = jnp.full_like(u, coefficients[-1])
    for coefficient in coefficients[-2::-1]:
        value = value * u + coefficient
    return value


def cos_sin(turns):
    r = turns - jnp.round(turns)
    u = r * r
    return horner(COS, u), r * horner(SIN, u)


def kernel(
    groups,
    inners,
    total_mics,
    bins_ref,
    signal_hbm,
    mic_hbm,
    grid_hbm,
    out_ref,
    signal,
    mic,
    grid,
    grid_cols,
    wide,
    spectra,
    received,
    cos_st,
    sin_st,
    excess,
    share,
    shares,
    value,
    values,
    signal_sem,
    mic_sem,
    grid_sem,
    x_send,
    x_recv,
    a_send,
    a_recv,
    b_send,
    b_recv,
):
    depth = groups // X_LO
    plane = X_LO * inners
    splits = plane // F
    snaps = signal.shape[0]
    mics = signal.shape[2]
    points = grid.shape[1]
    part = points // splits

    me_g = lax.axis_index("grp")
    me_i = lax.axis_index("inner")
    me_x = me_g // depth
    me_z = me_g % depth
    me_q = me_i * X_LO + me_x
    me_f = me_q // splits
    me_p = me_q % splits

    plane_peers = []
    for di in range(inners):
        for dx in range(X_LO):
            if di or dx:
                x = (me_x + dx) % X_LO
                i = (me_i + di) % inners
                plane_peers.append((x * depth + me_z, i, i * X_LO + x))
    depth_peers = [(me_x * depth + (me_z + dz) % depth, me_i) for dz in range(1, depth)]

    loads = []
    for s in range(snaps):
        loads.append(pltpu.make_async_copy(signal_hbm.at[s], signal.at[s], signal_sem.at[s]))
    for load in loads:
        load.start()
    grid_load = pltpu.make_async_copy(grid_hbm, grid, grid_sem)
    mic_load = pltpu.make_async_copy(mic_hbm, mic, mic_sem)
    grid_load.start()
    mic_load.start()

    barrier = pltpu.get_barrier_semaphore()
    for g, i, _ in plane_peers:
        pl.semaphore_signal(barrier, inc=1, device_id=(g, i), device_id_type=MESH)
    for g, i in depth_peers:
        pl.semaphore_signal(barrier, inc=1, device_id=(g, i), device_id_type=MESH)

    row = lax.broadcasted_iota(jnp.int32, (F, SAMPLES), 0)
    tick = lax.broadcasted_iota(jnp.int32, (F, SAMPLES), 1)
    bin_rows = jnp.zeros((F, SAMPLES), jnp.int32)
    for f in range(F):
        bin_rows = jnp.where(row == f, bins_ref[f], bin_rows)
    turns = lax.rem(bin_rows * tick, SAMPLES).astype(jnp.float32) * (1.0 / SAMPLES)
    cos_w, _ = cos_sin(tick.astype(jnp.float32) * (1.0 / SAMPLES))
    window = (0.5 - 0.5 * cos_w) * math.sqrt(8.0 / (3.0 * SAMPLES))
    cos_t, sin_t = cos_sin(turns)
    table = jnp.concatenate([window * cos_t, -(window * sin_t)], 0).astype(jnp.bfloat16)

    for s in range(snaps):
        loads[s].wait()
        wide[:, s, :] = jnp.dot(table, signal[s], preferred_element_type=jnp.float32)
    for f in range(F):
        spectra[f] = jnp.concatenate([wide[f], wide[F + f]], 0).astype(jnp.bfloat16)

    pl.semaphore_wait(barrier, len(plane_peers) + len(depth_peers))
    for g, i, q in plane_peers:
        pltpu.make_async_remote_copy(
            src_ref=spectra.at[q // splits],
            dst_ref=received.at[me_q],
            send_sem=x_send,
            recv_sem=x_recv,
            device_id=(g, i),
            device_id_type=MESH,
        ).start()
    pltpu.make_async_copy(spectra.at[me_f], received.at[me_q], x_recv).start()

    grid_load.wait()
    for axis in range(3):
        for tile in range(part // 128):
            at = pl.multiple_of(me_p * part + tile * 128, 128)
            line = grid[pl.ds(axis, 1), pl.ds(at, 128)]
            grid_cols[axis, pl.ds(tile * 128, 128), :] = jnp.transpose(
                jnp.broadcast_to(line, (128, 128))
            )
    mic_load.wait()
    rate = bins_ref[me_f].astype(jnp.float32) * TURNS_PER_METRE
    rows = 32

    def steer_block(block, carry):
        for tile in range(mics // 128):
            at = pl.multiple_of(block * mics + tile * 128, 128)
            mic_x = jnp.broadcast_to(mic[pl.ds(0, 1), pl.ds(at, 128)], (rows, 128))
            mic_y = jnp.broadcast_to(mic[pl.ds(1, 1), pl.ds(at, 128)], (rows, 128))
            mic_z = jnp.broadcast_to(mic[pl.ds(2, 1), pl.ds(at, 128)], (rows, 128))
            across = pl.ds(tile * 128, 128)
            for first in range(0, part, rows):
                down = pl.ds(first, rows)
                dx = grid_cols[0, down, :] - mic_x
                dy = grid_cols[1, down, :] - mic_y
                dz = grid_cols[2, down, :] - mic_z
                cos_a, sin_a = cos_sin(jnp.sqrt(dx * dx + dy * dy + dz * dz) * rate)
                cos_b = cos_a.astype(jnp.bfloat16)
                sin_b = sin_a.astype(jnp.bfloat16)
                cos_st[block, down, across] = cos_b
                sin_st[block, down, across] = sin_b
                cos_r = cos_b.astype(jnp.float32)
                sin_r = sin_b.astype(jnp.float32)
                excess[block, down, across] = (
                    (cos_r * cos_r - 1.0) + sin_r * sin_r
                ).astype(jnp.bfloat16)
        return carry

    lax.fori_loop(0, inners, steer_block, 0)

    pltpu.make_async_copy(received, received, x_recv).wait()

    lines = 2 * X_LO * snaps
    contract = (((1,), (1,)), ((), ()))

    def beam_block(block, carry):
        by_cos, by_sin, by_excess, energy = carry
        x = received[pl.ds(block * X_LO, X_LO)].reshape(lines, mics)
        wide_x = x.astype(jnp.float32)
        power = jnp.sum(wide_x * wide_x, axis=0, keepdims=True)
        power_b = jnp.broadcast_to(power, (16, mics)).astype(jnp.bfloat16)
        by_cos += lax.dot_general(x, cos_st[block], contract, preferred_element_type=jnp.float32)
        by_sin += lax.dot_general(x, sin_st[block], contract, preferred_element_type=jnp.float32)
        by_excess += lax.dot_general(
            power_b, excess[block], contract, preferred_element_type=jnp.float32
        )
        return by_cos, by_sin, by_excess, energy + power

    by_cos, by_sin, by_excess, energy = lax.fori_loop(
        0,
        inners,
        beam_block,
        (
            jnp.zeros((lines, part), jnp.float32),
            jnp.zeros((lines, part), jnp.float32),
            jnp.zeros((16, part), jnp.float32),
            jnp.zeros((1, mics), jnp.float32),
        ),
    )
    total = jnp.zeros((1, part), jnp.float32)
    for x in range(X_LO):
        re = slice(2 * x * snaps, (2 * x + 1) * snaps)
        im = slice((2 * x + 1) * snaps, (2 * x + 2) * snaps)
        beam_r = by_cos[re] - by_sin[im]
        beam_i = by_cos[im] + by_sin[re]
        total += jnp.sum(beam_r * beam_r + beam_i * beam_i, axis=0, keepdims=True)
    total -= jnp.sum(energy, axis=1, keepdims=True) + by_excess[0:1]

    halves = part // 128
    for h in range(halves):
        share[h : h + 1, :] = total[:, h * 128 : (h + 1) * 128]
    for g, i in depth_peers:
        pltpu.make_async_remote_copy(
            src_ref=share,
            dst_ref=shares.at[me_z],
            send_sem=a_send,
            recv_sem=a_recv,
            device_id=(g, i),
            device_id_type=MESH,
        ).start()
    shares[me_z] = share[...]
    pltpu.make_async_copy(
        shares.at[pl.ds(0, depth - 1)], shares.at[pl.ds(0, depth - 1)], a_recv
    ).wait()

    scale = 1.0 / (math.sqrt(groups * snaps) * total_mics)
    value[...] = jnp.sum(shares[...], axis=0) * scale
    for g, i, _ in plane_peers:
        pltpu.make_async_remote_copy(
            src_ref=value,
            dst_ref=values.at[me_q],
            send_sem=b_send,
            recv_sem=b_recv,
            device_id=(g, i),
            device_id_type=MESH,
        ).start()
    values[me_q] = value[...]
    pltpu.make_async_copy(
        values.at[pl.ds(0, plane - 1)], values.at[pl.ds(0, plane - 1)], b_recv
    ).wait()
    for q in range(plane):
        for h in range(halves):
            at = (q % splits) * part + h * 128
            out_ref[q // splits : q // splits + 1, at : at + 128] = values[q, h : h + 1, :]

    pltpu.make_async_copy(
        received.at[pl.ds(0, plane - 1)], received.at[pl.ds(0, plane - 1)], x_send
    ).wait()
    pltpu.make_async_copy(
        shares.at[pl.ds(0, depth - 1)], shares.at[pl.ds(0, depth - 1)], a_send
    ).wait()
    pltpu.make_async_copy(
        values.at[pl.ds(0, plane - 1)], values.at[pl.ds(0, plane - 1)], b_send
    ).wait()


def shards(groups, inners, signal, bins, mic_positions, grid_positions):
    snaps, _, mics = signal.shape
    total_mics = mic_positions.shape[1]
    points = grid_positions.shape[1]
    plane = X_LO * inners
    part = points // (plane // F)
    halves = part // 128
    bf16, f32 = jnp.bfloat16, jnp.float32
    dma = pltpu.SemaphoreType.DMA
    return pl.pallas_call(
        functools.partial(kernel, groups, inners, total_mics),
        out_shape=jax.ShapeDtypeStruct((F, points), f32),
        in_specs=[
            pl.BlockSpec(memory_space=pltpu.SMEM),
            pl.BlockSpec(memory_space=pltpu.HBM),
            pl.BlockSpec(memory_space=pltpu.HBM),
            pl.BlockSpec(memory_space=pltpu.HBM),
        ],
        out_specs=pl.BlockSpec(memory_space=pltpu.VMEM),
        scratch_shapes=[
            pltpu.VMEM(signal.shape, bf16),
            pltpu.VMEM(mic_positions.shape, f32),
            pltpu.VMEM(grid_positions.shape, f32),
            pltpu.VMEM((3, part, 128), f32),
            pltpu.VMEM((2 * F, snaps, mics), f32),
            pltpu.VMEM((F, 2 * snaps, mics), bf16),
            pltpu.VMEM((plane, 2 * snaps, mics), bf16),
            pltpu.VMEM((inners, part, mics), bf16),
            pltpu.VMEM((inners, part, mics), bf16),
            pltpu.VMEM((inners, part, mics), bf16),
            pltpu.VMEM((halves, 128), f32),
            pltpu.VMEM((groups // X_LO, halves, 128), f32),
            pltpu.VMEM((halves, 128), f32),
            pltpu.VMEM((plane, halves, 128), f32),
            dma((snaps,)),
        ]
        + [dma] * 8,
        compiler_params=pltpu.CompilerParams(
            collective_id=0, has_side_effects=True, vmem_limit_bytes=67_043_328
        ),
        name="beamform",
    )(bins, signal, mic_positions, grid_positions)


def solution(mesh):
    in_specs = (P("grp", None, "inner"), P(), P(), P())
    body = functools.partial(shards, mesh.shape["grp"], mesh.shape["inner"])
    return jax.shard_map(body, mesh=mesh, in_specs=in_specs, out_specs=P(), check_vma=False)
```

```python
import functools
import math

import jax
import jax.numpy as jnp
from jax import lax
from jax.experimental import pallas as pl
from jax.experimental.pallas import tpu as pltpu
from jax.sharding import PartitionSpec as P

SAMPLES = 1024
F = 8
X_LO = 2
TURNS_PER_METRE = (51200.0 / 343.0) / SAMPLES
MESH = pl.DeviceIdType.MESH

COS = (
    1.0,
    -19.73920440673828,
    64.93911743164062,
    -85.45014190673828,
    60.16762924194336,
    -25.967599868774414,
    6.528658390045166,
)
SIN = (
    6.283185005187988,
    -41.341590881347656,
    81.59994506835938,
    -76.61447143554688,
    41.3428840637207,
    -12.471243858337402,
)


def horner(coefficients, u):
    value = jnp.full_like(u, coefficients[-1])
    for coefficient in coefficients[-2::-1]:
        value = value * u + coefficient
    return value


def cos_sin(turns):
    r = turns - jnp.round(turns)
    u = r * r
    return horner(COS, u), r * horner(SIN, u)


def kernel(
    groups,
    inners,
    total_mics,
    bins_hbm,
    signal_hbm,
    mic_hbm,
    grid_hbm,
    out_ref,
    bins_ref,
    signal,
    mic,
    grid,
    grid_cols,
    wide,
    spectra,
    received,
    cos_st,
    sin_st,
    excess,
    share,
    shares,
    value,
    values,
    bins_sem,
    signal_sem,
    mic_sem,
    grid_sem,
    x_send,
    x_recv,
    a_send,
    a_recv,
    b_send,
    b_recv,
):
    depth = groups // X_LO
    plane = X_LO * inners
    splits = plane // F
    snaps = signal.shape[0]
    mics = signal.shape[2]
    points = grid.shape[1]
    part = points // splits

    me_g = lax.axis_index("grp")
    me_i = lax.axis_index("inner")
    me_x = me_g // depth
    me_z = me_g % depth
    me_q = me_i * X_LO + me_x
    me_f = me_q // splits
    me_p = me_q % splits

    me_c = me_i % 2
    me_h = me_i // 2 % 2
    me_y = me_i // 4
    ys = inners // 4
    plane_peers = []
    near, far = [], []
    for dy in range(ys):
        for dh in range(2):
            hops = min(dy, ys - dy) + (2 if dh else 1)
            for dc in range(2):
                i = (me_y + dy) % ys * 4 + (me_h + dh) % 2 * 2 + (me_c + dc) % 2
                (far if hops > 2 else near).append(i)
                for dx in range(X_LO):
                    if dy or dh or dc or dx:
                        x = (me_x + dx) % X_LO
                        away = min(dy, ys - dy) + (2 - dx if dh else dx)
                        plane_peers.append(
                            (away + dc, x * depth + me_z, i, i * X_LO + x, int(hops > 2))
                        )
    plane_peers.sort(key=lambda peer: -peer[0])
    plane_peers = [peer[1:] for peer in plane_peers]
    steps = sorted(range(1, depth), key=lambda dz: -min(dz, depth - dz))
    depth_peers = [(me_x * depth + (me_z + dz) % depth, me_i) for dz in steps]

    bins_load = pltpu.make_async_copy(bins_hbm, bins_ref, bins_sem)
    bins_load.start()
    loads = []
    for s in range(snaps):
        loads.append(pltpu.make_async_copy(signal_hbm.at[s], signal.at[s], signal_sem.at[s]))
    for load in loads:
        load.start()
    grid_load = pltpu.make_async_copy(grid_hbm, grid, grid_sem)
    mic_load = pltpu.make_async_copy(mic_hbm, mic, mic_sem)
    grid_load.start()
    mic_load.start()

    barrier = pltpu.get_barrier_semaphore()
    for g, i, _, _ in plane_peers:
        pl.semaphore_signal(barrier, inc=1, device_id=(g, i), device_id_type=MESH)
    for g, i in depth_peers:
        pl.semaphore_signal(barrier, inc=1, device_id=(g, i), device_id_type=MESH)

    row = lax.broadcasted_iota(jnp.int32, (F, SAMPLES), 0)
    tick = lax.broadcasted_iota(jnp.int32, (F, SAMPLES), 1)
    bins_load.wait()
    bin_rows = jnp.zeros((F, SAMPLES), jnp.int32)
    for f in range(F):
        bin_rows = jnp.where(row == f, bins_ref[f], bin_rows)
    turns = lax.rem(bin_rows * tick, SAMPLES).astype(jnp.float32) * (1.0 / SAMPLES)
    cos_w, _ = cos_sin(tick.astype(jnp.float32) * (1.0 / SAMPLES))
    window = (0.5 - 0.5 * cos_w) * math.sqrt(8.0 / (3.0 * SAMPLES))
    cos_t, sin_t = cos_sin(turns)
    table = jnp.concatenate([window * cos_t, -(window * sin_t)], 0).astype(jnp.bfloat16)

    for s in range(snaps):
        loads[s].wait()
        wide[:, s, :] = jnp.dot(table, signal[s], preferred_element_type=jnp.float32)
    for f in range(F):
        spectra[f] = jnp.concatenate([wide[f], wide[F + f]], 0).astype(jnp.bfloat16)

    pl.semaphore_wait(barrier, len(plane_peers) + len(depth_peers))
    for g, i, q, late in plane_peers:
        pltpu.make_async_remote_copy(
            src_ref=spectra.at[q // splits],
            dst_ref=received.at[me_q],
            send_sem=x_send,
            recv_sem=x_recv.at[late],
            device_id=(g, i),
            device_id_type=MESH,
        ).start()
    pltpu.make_async_copy(spectra.at[me_f], received.at[me_q], x_recv.at[0]).start()

    rate = bins_ref[me_f].astype(jnp.float32) * TURNS_PER_METRE
    grid_load.wait()
    for axis in range(3):
        for tile in range(part // 128):
            at = pl.multiple_of(me_p * part + tile * 128, 128)
            line = grid[pl.ds(axis, 1), pl.ds(at, 128)] * rate
            grid_cols[axis, pl.ds(tile * 128, 128), :] = jnp.transpose(
                jnp.broadcast_to(line, (128, 128))
            )
    mic_load.wait()
    rows = 32

    def steer_block(block, carry):
        for tile in range(mics // 128):
            at = pl.multiple_of(block * mics + tile * 128, 128)
            mic_x = jnp.broadcast_to(mic[pl.ds(0, 1), pl.ds(at, 128)] * rate, (rows, 128))
            mic_y = jnp.broadcast_to(mic[pl.ds(1, 1), pl.ds(at, 128)] * rate, (rows, 128))
            mic_z = jnp.broadcast_to(mic[pl.ds(2, 1), pl.ds(at, 128)] * rate, (rows, 128))
            across = pl.ds(tile * 128, 128)
            for first in range(0, part, rows):
                down = pl.ds(first, rows)
                dx = grid_cols[0, down, :] - mic_x
                dy = grid_cols[1, down, :] - mic_y
                dz = grid_cols[2, down, :] - mic_z
                squared = jnp.maximum(dx * dx + dy * dy + dz * dz, 1e-30)
                cos_a, sin_a = cos_sin(squared * lax.rsqrt(squared))
                cos_b = cos_a.astype(jnp.bfloat16)
                sin_b = sin_a.astype(jnp.bfloat16)
                cos_st[block, down, across] = cos_b
                sin_st[block, down, across] = sin_b
                cos_r = cos_b.astype(jnp.float32)
                sin_r = sin_b.astype(jnp.float32)
                excess[block, down, across] = (
                    (cos_r * cos_r - 1.0) + sin_r * sin_r
                ).astype(jnp.bfloat16)
        return carry

    lax.fori_loop(0, inners, steer_block, 0)

    lines = 2 * X_LO * snaps
    contract = (((1,), (1,)), ((), ()))
    by_cos = jnp.zeros((lines, part), jnp.float32)
    by_sin = jnp.zeros((lines, part), jnp.float32)
    by_excess = jnp.zeros((16, part), jnp.float32)
    energy = jnp.zeros((1, mics), jnp.float32)
    for late, blocks in enumerate((near, far)):
        if blocks:
            landed = received.at[pl.ds(0, X_LO * len(blocks))]
            pltpu.make_async_copy(landed, landed, x_recv.at[late]).wait()
        for block in blocks:
            x = received[pl.ds(block * X_LO, X_LO)].reshape(lines, mics)
            wide_x = x.astype(jnp.float32)
            power = jnp.sum(wide_x * wide_x, axis=0, keepdims=True)
            power_b = jnp.broadcast_to(power, (16, mics)).astype(jnp.bfloat16)
            by_cos += lax.dot_general(
                x, cos_st[block], contract, preferred_element_type=jnp.float32
            )
            by_sin += lax.dot_general(
                x, sin_st[block], contract, preferred_element_type=jnp.float32
            )
            by_excess += lax.dot_general(
                power_b, excess[block], contract, preferred_element_type=jnp.float32
            )
            energy += power
    total = jnp.zeros((1, part), jnp.float32)
    for x in range(X_LO):
        re = slice(2 * x * snaps, (2 * x + 1) * snaps)
        im = slice((2 * x + 1) * snaps, (2 * x + 2) * snaps)
        beam_r = by_cos[re] - by_sin[im]
        beam_i = by_cos[im] + by_sin[re]
        total += jnp.sum(beam_r * beam_r + beam_i * beam_i, axis=0, keepdims=True)
    total -= jnp.sum(energy, axis=1, keepdims=True) + by_excess[0:1]

    halves = part // 128
    for h in range(halves):
        share[h : h + 1, :] = total[:, h * 128 : (h + 1) * 128]
    for g, i in depth_peers:
        pltpu.make_async_remote_copy(
            src_ref=share,
            dst_ref=shares.at[me_z],
            send_sem=a_send,
            recv_sem=a_recv,
            device_id=(g, i),
            device_id_type=MESH,
        ).start()
    shares[me_z] = share[...]
    pltpu.make_async_copy(
        shares.at[pl.ds(0, depth - 1)], shares.at[pl.ds(0, depth - 1)], a_recv
    ).wait()

    scale = 1.0 / (math.sqrt(groups * snaps) * total_mics)
    value[...] = jnp.sum(shares[...], axis=0) * scale
    for g, i, _, _ in plane_peers:
        pltpu.make_async_remote_copy(
            src_ref=value,
            dst_ref=values.at[me_q],
            send_sem=b_send,
            recv_sem=b_recv,
            device_id=(g, i),
            device_id_type=MESH,
        ).start()
    values[me_q] = value[...]
    pltpu.make_async_copy(
        values.at[pl.ds(0, plane - 1)], values.at[pl.ds(0, plane - 1)], b_recv
    ).wait()
    for q in range(plane):
        for h in range(halves):
            at = (q % splits) * part + h * 128
            out_ref[q // splits : q // splits + 1, at : at + 128] = values[q, h : h + 1, :]

    pltpu.make_async_copy(
        received.at[pl.ds(0, plane - 1)], received.at[pl.ds(0, plane - 1)], x_send
    ).wait()
    pltpu.make_async_copy(
        shares.at[pl.ds(0, depth - 1)], shares.at[pl.ds(0, depth - 1)], a_send
    ).wait()
    pltpu.make_async_copy(
        values.at[pl.ds(0, plane - 1)], values.at[pl.ds(0, plane - 1)], b_send
    ).wait()


def shards(groups, inners, signal, bins, mic_positions, grid_positions):
    snaps, _, mics = signal.shape
    total_mics = mic_positions.shape[1]
    points = grid_positions.shape[1]
    plane = X_LO * inners
    part = points // (plane // F)
    halves = part // 128
    bf16, f32 = jnp.bfloat16, jnp.float32
    dma = pltpu.SemaphoreType.DMA
    return pl.pallas_call(
        functools.partial(kernel, groups, inners, total_mics),
        out_shape=jax.ShapeDtypeStruct((F, points), f32),
        in_specs=[
            pl.BlockSpec(memory_space=pltpu.HBM),
            pl.BlockSpec(memory_space=pltpu.HBM),
            pl.BlockSpec(memory_space=pltpu.HBM),
            pl.BlockSpec(memory_space=pltpu.HBM),
        ],
        out_specs=pl.BlockSpec(memory_space=pltpu.VMEM),
        scratch_shapes=[
            pltpu.SMEM(bins.shape, jnp.int32),
            pltpu.VMEM(signal.shape, bf16),
            pltpu.VMEM(mic_positions.shape, f32),
            pltpu.VMEM(grid_positions.shape, f32),
            pltpu.VMEM((3, part, 128), f32),
            pltpu.VMEM((2 * F, snaps, mics), f32),
            pltpu.VMEM((F, 2 * snaps, mics), bf16),
            pltpu.VMEM((plane, 2 * snaps, mics), bf16),
            pltpu.VMEM((inners, part, mics), bf16),
            pltpu.VMEM((inners, part, mics), bf16),
            pltpu.VMEM((inners, part, mics), bf16),
            pltpu.VMEM((halves, 128), f32),
            pltpu.VMEM((groups // X_LO, halves, 128), f32),
            pltpu.VMEM((halves, 128), f32),
            pltpu.VMEM((plane, halves, 128), f32),
            dma,
            dma((snaps,)),
            dma,
            dma,
            dma,
            dma((2,)),
        ]
        + [dma] * 4,
        compiler_params=pltpu.CompilerParams(
            collective_id=0, has_side_effects=True, vmem_limit_bytes=67_043_328
        ),
        name="beamform",
    )(bins, signal, mic_positions, grid_positions)


def solution(mesh):
    in_specs = (P("grp", None, "inner"), P(), P(), P())
    body = functools.partial(shards, mesh.shape["grp"], mesh.shape["inner"])
    return jax.shard_map(body, mesh=mesh, in_specs=in_specs, out_specs=P(), check_vma=False)
```
